512 devices in a mesh: tm: 16 (over z), det: 32 (over y, x, core).
Axes of the slice: x: 4, y: 4, z: 16, core: 2. Of those that a mesh axis runs over, the one named last changes fastest.
Arguments:
- noise: float32 [512, 65536], P('det', 'tm'), may hold values from -6 to 6
- factor: float32 [32, 512, 512], P('det', 'tm'), may hold values from -8 to 8, as said below
Outputs:
- correlated: float32 [512, 65536], P('det', 'tm')
The draws below stay inside these ranges and needn't reach their ends.
Inputs may be any that keep to these rules, and one draw needn't show every extreme that they name: factor[b] is lower triangular with a positive diagonal, and factor[b] equals factor[31 - b].
All inputs are finite; a program needn't handle non-finite values.
Results may differ from the reference program's by a relative error of at most 0.00007.
Values sent between devices are 32-bit elements; how exact they have to be, the bound alone decides.
A program may use at most 64 MiB of HBM per device.

```python
import math
import jax
import jax.numpy as jnp
from jax import lax

DET = 512
BW = 2048
NB = 32
NSAMP = 65536


def draw_factor(key, part):
    key_lower, key_diag = jax.random.split(key)
    half = NB // 2
    lower = jnp.clip(jax.random.normal(key_lower, (half, DET, DET), jnp.float32), -6.0, 6.0)
    diagonal = jax.random.uniform(key_diag, (half, DET), jnp.float32, 0.6, 1.4)
    lower = jnp.tril(lower, -1) * (0.8 / math.sqrt(DET))
    bands = jnp.arange(half, dtype=jnp.int32)
    folded = (bands + 1).astype(jnp.float32)
    amplitude = jnp.sqrt(NB / (2.0 * folded))
    matrix = lower + jnp.eye(DET, dtype=jnp.float32)[None, :, :] * diagonal[:, :, None]
    matrix = matrix * amplitude[:, None, None]
    return jnp.concatenate([matrix, matrix[::-1]], axis=0)


def level_of(own_key, extent, shards, least, high):
    factor_of, own = 1.0, jax.random.fold_in(own_key, 6)
    for dim, shards_of in shards:
        steps = jnp.exp(jax.random.uniform(jax.random.fold_in(own, dim), (shards_of,), jnp.float32, least / len(shards), high / len(shards)))
        factor_of = factor_of * jnp.repeat(steps, extent[dim] // shards_of).reshape([-1 if axis == dim else 1 for axis in range(len(extent))])
    return factor_of


def gaussian(key, dims, width, limit, shards=(), kind=jnp.bfloat16):
    entries = jax.random.normal(key, dims, jnp.float32) * width
    if len(shards) > 0:
        entries = level_of(key, dims, shards, -0.22, 0.18) * entries
    return jnp.clip(entries, min=-limit, max=limit).astype(kind)


def setup_inputs(seed: int = 0) -> dict:
    seeds = jax.random.split(jax.random.key(seed), 3)
    noise = gaussian(seeds[0], (DET, NSAMP), 1.0, 6.0, ((0, 32), (1, 16)), jnp.float32)
    factor = draw_factor(jax.random.fold_in(seeds[2], 71), 0)
    return dict(noise=noise, factor=factor)


def shift_phase(count):
    steps = jnp.arange(count, dtype=jnp.int32)
    return jnp.exp(-1j * jnp.pi * steps / count)


def forward_rows(values):
    count = values.shape[1]
    spectrum = jnp.fft.fft(values * shift_phase(count)[None, :], axis=1)
    return jnp.real(spectrum) - jnp.imag(spectrum)


def inverse_rows(values):
    count = values.shape[1]
    spectrum = jnp.fft.fft(values, axis=1) * shift_phase(count)[None, :]
    return (jnp.real(spectrum) - jnp.imag(spectrum)) / count


def reference(noise, factor):
    spectrum = forward_rows(noise).astype(jnp.float32)
    blocks = spectrum.reshape(DET, NB, BW)
    mixed = jnp.einsum('bij,jbk->ibk', factor, blocks, precision=lax.Precision.HIGHEST).reshape(DET, NSAMP)
    return inverse_rows(mixed).astype(jnp.float32)
```

```python
import math

import jax
import jax.numpy as jnp
import numpy as np
from jax import lax
from jax.experimental import pallas as pl
from jax.experimental.pallas import tpu as pltpu
from jax.sharding import PartitionSpec as P

MESH = pl.DeviceIdType.MESH
f32, bf16 = jnp.float32, jnp.bfloat16

PLANES = 16
GROUPS = 32
LANES = 128
ROWS = 512
DETS = 512
TOTAL = 65536


def split(values):
    high = values.astype(bf16)
    return high, (values - high.astype(f32)).astype(bf16)


def table_parts(table):
    high = table.astype(bf16)
    return high, (table - high.astype(np.float64)).astype(bf16)


def make_tables():
    q = np.arange(256)[:, None] + 0.5
    first = 2.0 * math.pi / 512 * (q * np.arange(512)[None, :])
    first = np.concatenate([np.cos(first), -np.sin(first)], axis=0)
    turn = 2.0 * math.pi / TOTAL * (q * np.arange(LANES)[None, :])
    pair = np.arange(16)[:, None]
    place = np.arange(4)[None, :]
    m = np.concatenate([4 * pair + place, 4 * (31 - pair) + place], axis=1)
    second = 2.0 * math.pi / LANES * ((m[:, :, None] * np.arange(LANES)) % LANES)
    cosines, sines = np.cos(second), np.sin(second)
    real_rows = np.concatenate([cosines, sines], axis=2)
    imag_rows = np.concatenate([-sines, cosines], axis=2)
    second = np.concatenate([real_rows, imag_rows], axis=1).reshape(256, 256)
    return (
        *table_parts(first),
        *table_parts(second),
        np.cos(turn).astype(np.float32),
        np.sin(turn).astype(np.float32),
    )


def product(left, right, dims):
    numbers = ((dims[:1], dims[1:]), ((), ()))
    total = None
    for a, b in ((0, 1), (1, 0), (0, 0)):
        term = lax.dot_general(left[a], right[b], numbers, preferred_element_type=f32)
        total = term if total is None else total + term
    return total


def rows_at(index, count):
    return pl.ds(pl.multiple_of(index * count, count), count)


def away(step, count):
    return count // 2 + (step + 1) // 2 * (1 - 2 * (step % 2))


class Exchange:
    def __init__(self, axis, count, rows, source, target, send, recv):
        self.axis, self.count, self.rows = axis, count, rows
        self.source, self.target, self.send, self.recv = source, target, send, recv

    def copy(self, peer, source_block, target_block, slot):
        return pltpu.make_async_remote_copy(
            src_ref=self.source.at[rows_at(source_block, self.rows)],
            dst_ref=self.target.at[rows_at(target_block, self.rows)],
            send_sem=self.send.at[peer],
            recv_sem=self.recv.at[slot],
            device_id={self.axis: peer},
            device_id_type=MESH,
        )

    def each(self, action):
        me = lax.axis_index(self.axis)

        def step(k, carry):
            action(me, lax.rem(me + away(k, self.count), self.count))
            return carry

        lax.fori_loop(0, self.count - 1, step, 0)

    def start(self, own=True):
        self.each(lambda me, peer: self.copy(peer, peer if own else me, me, me).start())
        if own:
            me = lax.axis_index(self.axis)
            here = rows_at(me, self.rows)
            self.target[here] = self.source[here]

    def wait_recv(self):
        self.each(lambda me, peer: self.copy(peer, me, peer, peer).wait_recv())

    def wait_send(self):
        self.each(lambda me, peer: self.copy(peer, peer, me, me).wait_send())


def kernel(
    noise, factor, first_high, first_low, second_high, second_low, cosines, sines, out,
    samples, x0, x1, x2, x3, x4, x5, x6, x7, x8, x9, x10, x11, flat, gathered, factor_high, factor_low,
    t_first_high, t_first_low, t_second_high, t_second_low, t_cos, t_sin,
    z_send, z_recv, d_send, d_recv, f_send, f_recv, part_send, part_recv, local_sem,
):
    plane = lax.axis_index("tm")
    group = lax.axis_index("det")
    upper = group // 16
    pair = group + upper * (31 - 2 * group)
    part_to = (pair, 2 * plane + upper)
    odd = lax.rem(group, 2)
    part_from = (group // 2, plane + odd * (31 - 2 * plane))
    stays = jnp.logical_and(part_to[0] == plane, part_to[1] == group)

    loads = [pltpu.make_async_copy(noise, samples, local_sem.at[0])]
    tables = (
        (first_high, t_first_high), (first_low, t_first_low), (second_high, t_second_high),
        (second_low, t_second_low), (cosines, t_cos), (sines, t_sin),
    )
    for n, (source, target) in enumerate(tables):
        loads.append(pltpu.make_async_copy(source, target, local_sem.at[n + 1]))
    for load in loads:
        load.start()

    barrier = pltpu.get_barrier_semaphore()

    def greet_planes(k, carry):
        peer = lax.rem(plane + away(k, PLANES), PLANES)
        pl.semaphore_signal(barrier, inc=1, device_id={"tm": peer}, device_id_type=MESH)
        return carry

    def greet_groups(k, carry):
        peer = lax.rem(group + away(k, GROUPS), GROUPS)
        pl.semaphore_signal(barrier, inc=1, device_id={"det": peer}, device_id_type=MESH)
        return carry

    lax.fori_loop(0, PLANES - 1, greet_planes, 0)
    lax.fori_loop(0, GROUPS - 1, greet_groups, 0)

    @pl.when(jnp.logical_not(stays))
    def _():
        for other in (part_to, part_from):
            pl.semaphore_signal(
                barrier, inc=1, device_id={"tm": other[0], "det": other[1]}, device_id_type=MESH
            )

    loads[0].wait()
    for j in range(32):
        x0[pl.ds(j, PLANES, stride=32), :] = samples[:, LANES * j : LANES * (j + 1)]

    @pl.when(stays)
    def _():
        pl.semaphore_wait(barrier, PLANES + GROUPS - 2)

    @pl.when(jnp.logical_not(stays))
    def _():
        pl.semaphore_wait(barrier, PLANES + GROUPS)

    def planes(n, source, target):
        return Exchange("tm", PLANES, 32, source, target, z_send.at[n], z_recv.at[n])

    def groups(n, source, target):
        return Exchange("det", GROUPS, 16, source, target, d_send.at[n], d_recv.at[n])

    to_detector = planes(0, x0, x1)
    to_detector.start()

    part = factor.at[0, pl.ds(pl.multiple_of(16 * upper, 16), 16)]
    part_copy = pltpu.make_async_remote_copy(
        src_ref=part,
        dst_ref=gathered.at[rows_at(part_to[1], 16)],
        send_sem=part_send,
        recv_sem=part_recv,
        device_id={"tm": part_to[0], "det": part_to[1]},
        device_id_type=MESH,
    )
    part_stays = pltpu.make_async_copy(part, gathered.at[rows_at(part_to[1], 16)], part_recv)

    @pl.when(jnp.logical_not(stays))
    def _():
        part_copy.start()
        pltpu.make_async_remote_copy(
            src_ref=part,
            dst_ref=gathered.at[rows_at(group, 16)],
            send_sem=part_send,
            recv_sem=part_recv,
            device_id={"tm": part_from[0], "det": part_from[1]},
            device_id_type=MESH,
        ).wait_recv()

    @pl.when(stays)
    def _():
        part_stays.start()
        part_stays.wait()

    factor_rows = Exchange("det", GROUPS, 16, gathered, gathered, f_send, f_recv)
    factor_rows.start(own=False)

    for load in loads[1:]:
        load.wait()
    first = (t_first_high[...], t_first_low[...])
    to_detector.wait_recv()

    samples_of = split(x1[...])
    spectrum = product(first, samples_of, (1, 0))
    real, imag = spectrum[:256], spectrum[256:]
    turned = jnp.concatenate(
        [real * t_cos[...] + imag * t_sin[...], imag * t_cos[...] - real * t_sin[...]], axis=1
    )
    bins = product((t_second_high[...], t_second_low[...]), split(turned), (1, 1))
    for p in range(PLANES):
        for half in range(2):
            x2[32 * p + 16 * half : 32 * p + 16 * half + 16, :] = bins[
                16 * p : 16 * p + 16, LANES * half : LANES * half + LANES
            ]

    to_pair = planes(1, x2, x3)
    to_pair.start()
    factor_rows.wait_recv()
    high, low = split(gathered[...])
    factor_high[...] = high
    factor_low[...] = low
    to_pair.wait_recv()

    for g in range(GROUPS):
        x4[16 * g : 16 * g + 16, :] = x3[pl.ds(g, PLANES, stride=GROUPS), :]
    to_bins = groups(0, x4, x5)
    to_bins.start()
    to_bins.wait_recv()

    x6[...] = product((factor_high[...], factor_low[...]), split(x5[...]), (1, 0))

    from_bins = groups(1, x6, x7)
    from_bins.start()
    from_bins.wait_recv()
    for p in range(PLANES):
        x8[32 * p : 32 * p + 32, :] = x7[pl.ds(p, GROUPS, stride=PLANES), :]

    from_pair = planes(2, x8, x9)
    from_pair.start()
    from_pair.wait_recv()

    for p in range(PLANES):
        for half in range(2):
            flat[16 * p : 16 * p + 16, LANES * half : LANES * half + LANES] = x9[
                32 * p + 16 * half : 32 * p + 16 * half + 16, :
            ]
    back = product(split(flat[...]), (t_second_high[...], t_second_low[...]), (0, 0))
    real, imag = back[:, :LANES], back[:, LANES:]
    turned = jnp.concatenate(
        [real * t_cos[...] - imag * t_sin[...], imag * t_cos[...] + real * t_sin[...]], axis=0
    )
    x10[...] = product(first, split(turned), (0, 0)) * (2.0 / TOTAL)

    to_block = planes(3, x10, x11)
    to_block.start()
    to_block.wait_recv()
    for j in range(32):
        out[:, LANES * j : LANES * (j + 1)] = x11[pl.ds(j, PLANES, stride=32), :]

    @pl.when(jnp.logical_not(stays))
    def _():
        part_copy.wait_send()

    factor_rows.wait_send()
    for exchange in (to_detector, to_pair, to_bins, from_bins, from_pair, to_block):
        exchange.wait_send()


def local(noise, factor):
    any_space = pl.BlockSpec(memory_space=pl.ANY)
    block = pltpu.VMEM((ROWS, LANES), f32)
    return pl.pallas_call(
        kernel,
        out_shape=jax.ShapeDtypeStruct((PLANES, ROWS * LANES // PLANES), f32),
        in_specs=[any_space] * 8,
        out_specs=pl.BlockSpec(memory_space=pltpu.VMEM),
        scratch_shapes=[
            pltpu.VMEM((PLANES, ROWS * LANES // PLANES), f32),
            *[block] * 12,
            pltpu.VMEM((256, 256), f32),
            pltpu.VMEM((DETS, DETS), f32),
            pltpu.VMEM((DETS, DETS), bf16),
            pltpu.VMEM((DETS, DETS), bf16),
            pltpu.VMEM((512, 512), bf16),
            pltpu.VMEM((512, 512), bf16),
            pltpu.VMEM((256, 256), bf16),
            pltpu.VMEM((256, 256), bf16),
            pltpu.VMEM((256, LANES), f32),
            pltpu.VMEM((256, LANES), f32),
            pltpu.SemaphoreType.DMA((4, PLANES)),
            pltpu.SemaphoreType.DMA((4, PLANES)),
            pltpu.SemaphoreType.DMA((2, GROUPS)),
            pltpu.SemaphoreType.DMA((2, GROUPS)),
            pltpu.SemaphoreType.DMA((GROUPS,)),
            pltpu.SemaphoreType.DMA((GROUPS,)),
            pltpu.SemaphoreType.DMA,
            pltpu.SemaphoreType.DMA,
            pltpu.SemaphoreType.DMA((8,)),
        ],
        compiler_params=pltpu.CompilerParams(collective_id=0, has_side_effects=True),
        name="mix",
    )(noise, factor, *make_tables())


def solution(mesh):
    in_specs = (P("det", "tm"), P("det", "tm", None))
    return jax.shard_map(local, mesh=mesh, in_specs=in_specs, out_specs=P("det", "tm"), check_vma=False)
```

```python
import math

import jax
import jax.numpy as jnp
import numpy as np
from jax import lax
from jax.experimental import pallas as pl
from jax.experimental.pallas import tpu as pltpu
from jax.sharding import PartitionSpec as P

MESH = pl.DeviceIdType.MESH
f32, bf16 = jnp.float32, jnp.bfloat16

PLANES = 16
GROUPS = 32
LANES = 128
ROWS = 512
DETS = 512
TOTAL = 65536
CHUNKS = 4


def split(values):
    high = values.astype(bf16)
    return high, (values - high.astype(f32)).astype(bf16)


def table_parts(table):
    high = table.astype(bf16)
    return high, (table - high.astype(np.float64)).astype(bf16)


def make_tables():
    q = np.arange(256)[:, None] + 0.5
    first = 2.0 * math.pi / 512 * (q * np.arange(512)[None, :])
    first = np.concatenate([np.cos(first), -np.sin(first)], axis=0)
    turn = 2.0 * math.pi / TOTAL * (q * np.arange(LANES)[None, :])
    pair = np.arange(16)[:, None]
    place = np.arange(4)[None, :]
    m = np.concatenate([4 * pair + place, 4 * (31 - pair) + place], axis=1)
    second = 2.0 * math.pi / LANES * ((m[:, :, None] * np.arange(LANES)) % LANES)
    cosines, sines = np.cos(second), np.sin(second)
    real_rows = np.concatenate([cosines, sines], axis=2)
    imag_rows = np.concatenate([-sines, cosines], axis=2)
    second = np.concatenate([real_rows, imag_rows], axis=1).reshape(256, 256)
    return (
        *table_parts(first),
        *table_parts(second),
        np.cos(turn).astype(np.float32),
        np.sin(turn).astype(np.float32),
    )


def product(left, right, dims):
    numbers = ((dims[:1], dims[1:]), ((), ()))
    total = None
    for a, b in ((0, 1), (1, 0), (0, 0)):
        term = lax.dot_general(left[a], right[b], numbers, preferred_element_type=f32)
        total = term if total is None else total + term
    return total


def rows_at(index, count):
    return pl.ds(pl.multiple_of(index * count, count), count)


def away(step, count):
    return count // 2 + (step + 1) // 2 * (1 - 2 * (step % 2))


class Exchange:
    def __init__(self, axis, count, rows, chunks, source, target, send, recv):
        self.axis, self.count, self.rows, self.chunks = axis, count, rows, chunks
        self.source, self.target, self.send, self.recv = source, target, send, recv

    def block(self, ref, index, chunk):
        return ref.at[rows_at(index * self.chunks + chunk, self.rows)]

    def copy(self, peer, source_block, target_block, slot, chunk):
        return pltpu.make_async_remote_copy(
            src_ref=self.block(self.source, source_block, chunk),
            dst_ref=self.block(self.target, target_block, chunk),
            send_sem=self.send.at[peer, chunk],
            recv_sem=self.recv.at[slot, chunk],
            device_id={self.axis: peer},
            device_id_type=MESH,
        )

    def each(self, action):
        me = lax.axis_index(self.axis)

        def step(k, carry):
            action(me, lax.rem(me + away(k, self.count), self.count))
            return carry

        lax.fori_loop(0, self.count - 1, step, 0, unroll=True)

    def start(self, chunk=0):
        self.each(lambda me, peer: self.copy(peer, peer, me, me, chunk).start())
        me = lax.axis_index(self.axis)
        here = rows_at(me * self.chunks + chunk, self.rows)
        self.target[here] = self.source[here]

    def wait_recv(self, chunk=0):
        self.each(lambda me, peer: self.copy(peer, me, peer, peer, chunk).wait_recv())

    def wait_send(self):
        for chunk in range(self.chunks):
            self.each(lambda me, peer: self.copy(peer, peer, me, me, chunk).wait_send())


def kernel(
    noise, factor, first_high, first_low, second_high, second_low, cosines, sines, out,
    samples, x0, x1, x2, x3, x4, x5, x6, x7, x8, x9, x10, x11, flat, turned_high, turned_low, gathered, factor_high, factor_low,
    t_first_high, t_first_low, t_second_high, t_second_low, t_cos, t_sin,
    z_send, z_recv, c_send, c_recv, d_send, d_recv, f_send, f_recv, part_send, part_recv, local_sem,
):
    plane = lax.axis_index("tm")
    group = lax.axis_index("det")
    upper = group // 16
    core = lax.rem(group, 2)
    chip = group // 2
    kind = lax.rem(group, CHUNKS)
    pair = group + upper * (31 - 2 * group)
    part_to = (pair, 2 * plane + upper)
    part_from = (chip, plane + core * (31 - 2 * plane))
    stays = jnp.logical_and(part_to[0] == plane, part_to[1] == group)
    leaves = jnp.logical_not(stays)

    loads = [pltpu.make_async_copy(noise, samples, local_sem.at[0])]
    tables = (
        (first_high, t_first_high), (first_low, t_first_low), (second_high, t_second_high),
        (second_low, t_second_low), (cosines, t_cos), (sines, t_sin),
    )
    for n, (source, target) in enumerate(tables):
        loads.append(pltpu.make_async_copy(source, target, local_sem.at[n + 1]))
    loads[0].start()

    barrier = pltpu.get_barrier_semaphore()

    def greet_planes(k, carry):
        peer = lax.rem(plane + away(k, PLANES), PLANES)
        pl.semaphore_signal(barrier, inc=1, device_id={"tm": peer}, device_id_type=MESH)
        return carry

    def greet_groups(k, carry):
        peer = lax.rem(group + away(k, GROUPS), GROUPS)
        pl.semaphore_signal(barrier, inc=1, device_id={"det": peer}, device_id_type=MESH)
        return carry

    lax.fori_loop(0, PLANES - 1, greet_planes, 0, unroll=True)

    @pl.when(leaves)
    def _():
        for other in (part_to, part_from):
            pl.semaphore_signal(
                barrier, inc=1, device_id={"tm": other[0], "det": other[1]}, device_id_type=MESH
            )

    lax.fori_loop(0, GROUPS - 1, greet_groups, 0, unroll=True)
    for load in loads[1:]:
        load.start()

    loads[0].wait()
    for j in range(32):
        x0[pl.ds(j, PLANES, stride=32), :] = samples[:, LANES * j : LANES * (j + 1)]

    @pl.when(stays)
    def _():
        pl.semaphore_wait(barrier, PLANES + GROUPS - 2)

    @pl.when(leaves)
    def _():
        pl.semaphore_wait(barrier, PLANES + GROUPS)

    part = factor.at[0, pl.ds(pl.multiple_of(16 * upper, 16), 16)]

    def factor_block(index):
        return gathered.at[index // 2, pl.ds(pl.multiple_of(16 * lax.rem(index, 2), 16), 16)]

    part_copy = pltpu.make_async_remote_copy(
        src_ref=part,
        dst_ref=factor_block(part_to[1]),
        send_sem=part_send.at[0],
        recv_sem=part_recv.at[0],
        device_id={"tm": part_to[0], "det": part_to[1]},
        device_id_type=MESH,
    )
    part_stays = pltpu.make_async_copy(part, factor_block(group), part_recv.at[0])

    @pl.when(leaves)
    def _():
        part_copy.start()

    @pl.when(stays)
    def _():
        part_stays.start()

    to_detector = Exchange("tm", PLANES, 32, 1, x0, x1, z_send.at[0], z_recv.at[0])
    to_detector.start()

    def chip_copy(other, block):
        return pltpu.make_async_remote_copy(
            src_ref=factor_block(2 * block + core),
            dst_ref=factor_block(2 * block + core),
            send_sem=f_send.at[other],
            recv_sem=f_recv.at[block],
            device_id={"det": 2 * other + core},
            device_id_type=MESH,
        )

    def each_chip(action):
        def step(k, carry):
            action(lax.rem(chip + away(k, 16), 16))
            return carry

        lax.fori_loop(0, 15, step, 0, unroll=True)

    def half_of(index):
        return gathered.at[:, pl.ds(pl.multiple_of(16 * index, 16), 16)]

    def core_copy(half):
        return pltpu.make_async_remote_copy(
            src_ref=half_of(half),
            dst_ref=half_of(half),
            send_sem=part_send.at[1],
            recv_sem=part_recv.at[1],
            device_id={"det": group + 1 - 2 * core},
            device_id_type=MESH,
        )

    @pl.when(leaves)
    def _():
        pltpu.make_async_remote_copy(
            src_ref=part,
            dst_ref=factor_block(group),
            send_sem=part_send.at[0],
            recv_sem=part_recv.at[0],
            device_id={"tm": part_from[0], "det": part_from[1]},
            device_id_type=MESH,
        ).wait_recv()

    @pl.when(stays)
    def _():
        part_stays.wait()

    each_chip(lambda other: chip_copy(other, chip).start())

    for load in loads[1:]:
        load.wait()
    to_detector.wait_recv()

    to_pair = Exchange("tm", PLANES, 8, CHUNKS, x2, x3, c_send.at[0], c_recv.at[0])
    from_pair = Exchange("tm", PLANES, 8, CHUNKS, x8, x9, c_send.at[1], c_recv.at[1])

    samples_of = split(x1[...])
    for half in range(2):
        parts = []
        for offset in (128 * half, 256 + 128 * half):
            rows = slice(offset, offset + 128)
            parts.append(product((t_first_high[rows], t_first_low[rows]), samples_of, (1, 0)))
        real, imag = parts
        rows = slice(128 * half, 128 * half + 128)
        cos, sin = t_cos[rows], t_sin[rows]
        turned = jnp.concatenate([real * cos + imag * sin, imag * cos - real * sin], axis=1)
        bins = product((t_second_high[...], t_second_low[...]), split(turned), (1, 1))
        for p in range(PLANES):
            x2[32 * p + 16 * half : 32 * p + 16 * half + 16, :] = bins[16 * p : 16 * p + 16]
        to_pair.start(2 * half)
        to_pair.start(2 * half + 1)

    def bins_copy(n, source, target, peer, source_block, target_block, slot):
        return pltpu.make_async_remote_copy(
            src_ref=source.at[rows_at(source_block, 16)],
            dst_ref=target.at[rows_at(target_block, 16)],
            send_sem=d_send.at[n, peer],
            recv_sem=d_recv.at[n, slot],
            device_id={"det": peer},
            device_id_type=MESH,
        )

    def each_group(action):
        def step(k, carry):
            action(lax.rem(group + away(k, GROUPS), GROUPS))
            return carry

        lax.fori_loop(0, GROUPS - 1, step, 0, unroll=True)

    def spread(chunk):
        to_pair.wait_recv(chunk)
        for u in range(8):
            peer = 4 * u + chunk
            x4[rows_at(peer, 16)] = x3[pl.ds(8 * chunk + u, PLANES, stride=32), :]

        def step(u, carry):
            peer = 4 * lax.rem(group // 4 + u + 4, 8) + chunk

            @pl.when(peer != group)
            def _():
                bins_copy(0, x4, x5, peer, peer, group, group).start()

            return carry

        lax.fori_loop(0, 8, step, 0, unroll=True)

        @pl.when(kind == chunk)
        def _():
            x5[rows_at(group, 16)] = x4[rows_at(group, 16)]

    def factor_ready():
        each_chip(lambda other: chip_copy(other, other).wait_recv())
        core_copy(core).start()
        core_copy(1 - core).wait_recv()
        high, low = split(gathered[...].reshape(DETS, DETS))
        factor_high[...] = high
        factor_low[...] = low

    def mix():
        each_group(lambda other: bins_copy(0, x4, x5, other, other, other, other).wait_recv())
        high, low = split(x5[...])
        for quarter in range(4):
            rows = slice(128 * quarter, 128 * quarter + 128)
            depth = 128 * quarter + 128
            x6[rows] = product(
                (factor_high[rows, :depth], factor_low[rows, :depth]), (high[:depth], low[:depth]), (1, 0)
            )

            def step(u, carry):
                peer = 8 * quarter + u

                @pl.when(peer != group)
                def _():
                    bins_copy(1, x6, x7, peer, peer, group, group).start()

                return carry

            lax.fori_loop(0, 8, step, 0, unroll=True)
        x7[rows_at(group, 16)] = x6[rows_at(group, 16)]

    def gather(chunk):
        def step(u, carry):
            other = 4 * u + chunk

            @pl.when(other != group)
            def _():
                bins_copy(1, x6, x7, other, other, other, other).wait_recv()

            return carry

        lax.fori_loop(0, 8, step, 0, unroll=True)
        for u in range(8):
            x8[pl.ds(8 * chunk + u, PLANES, stride=32), :] = x7[rows_at(4 * u + chunk, 16)]
        from_pair.start(chunk)

    factor_ready()

    def stage(n, carry):
        @pl.when(n < CHUNKS)
        def _():
            spread(n)

        @pl.when(kind == n - 1)
        def _():
            mix()

        @pl.when(n >= 2)
        def _():
            gather(n - 2)

        return carry

    lax.fori_loop(0, CHUNKS + 2, stage, 0)

    for half in range(2):
        from_pair.wait_recv(2 * half)
        from_pair.wait_recv(2 * half + 1)
        for p in range(PLANES):
            flat[16 * p : 16 * p + 16] = x9[32 * p + 16 * half : 32 * p + 16 * half + 16, :]
        back = product(split(flat[...]), (t_second_high[...], t_second_low[...]), (0, 0))
        real, imag = back[:, :LANES], back[:, LANES:]
        rows = slice(128 * half, 128 * half + 128)
        cos, sin = t_cos[rows], t_sin[rows]
        for offset, turned in (
            (128 * half, real * cos - imag * sin),
            (256 + 128 * half, imag * cos + real * sin),
        ):
            high, low = split(turned * (2.0 / TOTAL))
            turned_high[offset : offset + 128] = high
            turned_low[offset : offset + 128] = low
    x10[...] = product(
        (t_first_high[...], t_first_low[...]), (turned_high[...], turned_low[...]), (0, 0)
    )

    to_block = Exchange("tm", PLANES, 32, 1, x10, x11, z_send.at[1], z_recv.at[1])
    to_block.start()
    to_block.wait_recv()
    for j in range(32):
        out[:, LANES * j : LANES * (j + 1)] = x11[pl.ds(j, PLANES, stride=32), :]

    @pl.when(leaves)
    def _():
        part_copy.wait_send()

    each_chip(lambda other: chip_copy(other, chip).wait_send())
    core_copy(core).wait_send()
    each_group(lambda other: bins_copy(0, x4, x5, other, other, group, group).wait_send())
    each_group(lambda other: bins_copy(1, x6, x7, other, other, group, group).wait_send())
    for exchange in (to_detector, to_pair, from_pair, to_block):
        exchange.wait_send()


def local(noise, factor):
    any_space = pl.BlockSpec(memory_space=pl.ANY)
    block = pltpu.VMEM((ROWS, LANES), f32)
    return pl.pallas_call(
        kernel,
        out_shape=jax.ShapeDtypeStruct((PLANES, ROWS * LANES // PLANES), f32),
        in_specs=[any_space] * 8,
        out_specs=pl.BlockSpec(memory_space=pltpu.VMEM),
        scratch_shapes=[
            pltpu.VMEM((PLANES, ROWS * LANES // PLANES), f32),
            *[block] * 12,
            pltpu.VMEM((256, LANES), f32),
            pltpu.VMEM((ROWS, LANES), bf16),
            pltpu.VMEM((ROWS, LANES), bf16),
            pltpu.VMEM((16, 32, DETS), f32),
            pltpu.VMEM((DETS, DETS), bf16),
            pltpu.VMEM((DETS, DETS), bf16),
            pltpu.VMEM((512, 512), bf16),
            pltpu.VMEM((512, 512), bf16),
            pltpu.VMEM((256, 256), bf16),
            pltpu.VMEM((256, 256), bf16),
            pltpu.VMEM((256, LANES), f32),
            pltpu.VMEM((256, LANES), f32),
            pltpu.SemaphoreType.DMA((2, PLANES, 1)),
            pltpu.SemaphoreType.DMA((2, PLANES, 1)),
            pltpu.SemaphoreType.DMA((2, PLANES, CHUNKS)),
            pltpu.SemaphoreType.DMA((2, PLANES, CHUNKS)),
            pltpu.SemaphoreType.DMA((2, GROUPS)),
            pltpu.SemaphoreType.DMA((2, GROUPS)),
            pltpu.SemaphoreType.DMA((16,)),
            pltpu.SemaphoreType.DMA((16,)),
            pltpu.SemaphoreType.DMA((2,)),
            pltpu.SemaphoreType.DMA((2,)),
            pltpu.SemaphoreType.DMA((8,)),
        ],
        compiler_params=pltpu.CompilerParams(collective_id=0, has_side_effects=True),
        name="mix",
    )(noise, factor, *make_tables())


def solution(mesh):
    in_specs = (P("det", "tm"), P("det", "tm", None))
    return jax.shard_map(local, mesh=mesh, in_specs=in_specs, out_specs=P("det", "tm"), check_vma=False)
```

```python
import math

import jax
import jax.numpy as jnp
import numpy as np
from jax import lax
from jax.experimental import pallas as pl
from jax.experimental.pallas import tpu as pltpu
from jax.sharding import PartitionSpec as P

MESH = pl.DeviceIdType.MESH
f32, bf16 = jnp.float32, jnp.bfloat16

PLANES = 16
GROUPS = 32
LANES = 128
ROWS = 512
DETS = 512
TOTAL = 65536
CHUNKS = 4


def split(values):
    high = values.astype(bf16)
    return high, (values - high.astype(f32)).astype(bf16)


def table_parts(table):
    high = table.astype(bf16)
    return high, (table - high.astype(np.float64)).astype(bf16)


def make_tables():
    q = np.arange(256)[:, None] + 0.5
    first = 2.0 * math.pi / 512 * (q * np.arange(512)[None, :])
    first = np.concatenate([np.cos(first), -np.sin(first)], axis=0)
    turn = 2.0 * math.pi / TOTAL * (q * np.arange(LANES)[None, :])
    pair = np.arange(16)[:, None]
    place = np.arange(4)[None, :]
    m = np.concatenate([4 * pair + place, 4 * (31 - pair) + place], axis=1)
    second = 2.0 * math.pi / LANES * ((m[:, :, None] * np.arange(LANES)) % LANES)
    cosines, sines = np.cos(second), np.sin(second)
    real_rows = np.concatenate([cosines, sines], axis=2)
    imag_rows = np.concatenate([-sines, cosines], axis=2)
    second = np.concatenate([real_rows, imag_rows], axis=1).reshape(256, 256)
    return (
        *table_parts(first),
        *table_parts(second),
        np.cos(turn).astype(np.float32),
        np.sin(turn).astype(np.float32),
    )


def product(left, right, dims):
    numbers = ((dims[:1], dims[1:]), ((), ()))
    total = None
    for a, b in ((0, 1), (1, 0), (0, 0)):
        term = lax.dot_general(left[a], right[b], numbers, preferred_element_type=f32)
        total = term if total is None else total + term
    return total


def rows_at(index, count):
    return pl.ds(pl.multiple_of(index * count, count), count)


def away(step, count):
    return count // 2 + (step + 1) // 2 * (1 - 2 * (step % 2))


def await_rows(ref, sem):
    pltpu.make_async_copy(ref, ref, sem).wait()


class Exchange:
    def __init__(self, axis, count, rows, chunks, source, target, send, recv):
        self.axis, self.count, self.rows, self.chunks = axis, count, rows, chunks
        self.source, self.target, self.send, self.recv = source, target, send, recv

    def start(self, chunk=0):
        me = lax.axis_index(self.axis)
        here = rows_at(me * self.chunks + chunk, self.rows)

        def step(k, carry):
            peer = lax.rem(me + away(k, self.count), self.count)
            pltpu.make_async_remote_copy(
                src_ref=self.source.at[rows_at(peer * self.chunks + chunk, self.rows)],
                dst_ref=self.target.at[here],
                send_sem=self.send,
                recv_sem=self.recv.at[chunk],
                device_id={self.axis: peer},
                device_id_type=MESH,
            ).start()
            return carry

        lax.fori_loop(0, self.count - 1, step, 0, unroll=True)
        self.target[here] = self.source[here]

    def wait_recv(self, chunk=0):
        await_rows(self.target.at[0 : (self.count - 1) * self.rows], self.recv.at[chunk])

    def wait_send(self):
        await_rows(self.source.at[0 : (self.count - 1) * self.rows * self.chunks], self.send)


def kernel(
    noise, factor, first_high, first_low, second_high, second_low, cosines, sines, out,
    samples, x0, x1, x2, x3, x4, x5, x6, x7, x8, x9, x10, x11, flat, turned_high, turned_low, gathered, factor_high, factor_low,
    t_first_high, t_first_low, t_second_high, t_second_low, t_cos, t_sin,
    z_send, z_recv, c_send, c_recv, d_send, d_recv, f_send, f_recv, twin_send, twin_recv, part_send, part_recv, local_sem,
):
    plane = lax.axis_index("tm")
    group = lax.axis_index("det")
    upper = group // 16
    core = lax.rem(group, 2)
    chip = group // 2
    kind = lax.rem(group, CHUNKS)
    pair = group + upper * (31 - 2 * group)
    sent = 2 * plane + upper
    part_to = (pair, 2 * lax.rem(plane + pair, PLANES) + upper)
    mine = lax.rem(chip - plane + PLANES, PLANES)
    part_from = (mine, plane + core * (31 - 2 * plane))
    stays = jnp.logical_and(part_to[0] == plane, part_to[1] == group)
    leaves = jnp.logical_not(stays)

    loads = [pltpu.make_async_copy(noise, samples, local_sem.at[0])]
    tables = (
        (first_high, t_first_high), (first_low, t_first_low), (second_high, t_second_high),
        (second_low, t_second_low), (cosines, t_cos), (sines, t_sin),
    )
    for n, (source, target) in enumerate(tables):
        loads.append(pltpu.make_async_copy(source, target, local_sem.at[n + 1]))
    loads[0].start()

    barrier = pltpu.get_barrier_semaphore()

    def greet_planes(k, carry):
        peer = lax.rem(plane + away(k, PLANES), PLANES)
        pl.semaphore_signal(barrier, inc=1, device_id={"tm": peer}, device_id_type=MESH)
        return carry

    def greet_groups(k, carry):
        peer = lax.rem(group + away(k, GROUPS), GROUPS)
        pl.semaphore_signal(barrier, inc=1, device_id={"det": peer}, device_id_type=MESH)
        return carry

    lax.fori_loop(0, PLANES - 1, greet_planes, 0, unroll=True)

    @pl.when(leaves)
    def _():
        for other in (part_to, part_from):
            pl.semaphore_signal(
                barrier, inc=1, device_id={"tm": other[0], "det": other[1]}, device_id_type=MESH
            )

    lax.fori_loop(0, GROUPS - 1, greet_groups, 0, unroll=True)
    for load in loads[1:]:
        load.start()

    loads[0].wait()
    for j in range(32):
        x0[pl.ds(j, PLANES, stride=32), :] = samples[:, LANES * j : LANES * (j + 1)]

    @pl.when(stays)
    def _():
        pl.semaphore_wait(barrier, PLANES + GROUPS - 2)

    @pl.when(leaves)
    def _():
        pl.semaphore_wait(barrier, PLANES + GROUPS)

    to_detector = Exchange("tm", PLANES, 32, 1, x0, x1, z_send.at[0], z_recv.at[pl.ds(0, 1)])
    to_detector.start()

    part = factor.at[0, pl.ds(pl.multiple_of(16 * upper, 16), 16)]

    def factor_block(index):
        return gathered.at[index // 2, pl.ds(pl.multiple_of(16 * lax.rem(index, 2), 16), 16)]

    def part_copy(quarter, index, other):
        columns = pl.ds(0, 128 * quarter + 128)
        return pltpu.make_async_remote_copy(
            src_ref=part.at[:, columns],
            dst_ref=factor_block(index).at[:, columns],
            send_sem=part_send,
            recv_sem=part_recv,
            device_id={"tm": other[0], "det": other[1]},
            device_id_type=MESH,
        )

    part_stays = pltpu.make_async_copy(part, factor_block(sent), part_recv)

    def each_quarter(of, action):
        for quarter in range(4):

            @pl.when(of // 4 == quarter)
            def _():
                action(quarter)

    @pl.when(leaves)
    def _():
        each_quarter(plane, lambda quarter: part_copy(quarter, sent, part_to).start())

    @pl.when(stays)
    def _():
        part_stays.start()

    def chip_copy(quarter, other, block):
        columns = pl.ds(0, 128 * quarter + 128)
        return pltpu.make_async_remote_copy(
            src_ref=factor_block(2 * block + core).at[:, columns],
            dst_ref=factor_block(2 * block + core).at[:, columns],
            send_sem=f_send,
            recv_sem=f_recv.at[block],
            device_id={"det": 2 * other + core},
            device_id_type=MESH,
        )

    def to_chips(quarter):
        def step(k, carry):
            chip_copy(quarter, lax.rem(chip + away(k, 16), 16), mine).start()
            return carry

        lax.fori_loop(0, 15, step, 0)

    def core_copy(half, quarter):
        ref = gathered.at[
            4 * quarter : 4 * quarter + 4,
            pl.ds(pl.multiple_of(16 * half, 16), 16),
            0 : 128 * quarter + 128,
        ]
        return pltpu.make_async_remote_copy(
            src_ref=ref,
            dst_ref=ref,
            send_sem=twin_send.at[quarter],
            recv_sem=twin_recv.at[quarter],
            device_id={"det": group + 1 - 2 * core},
            device_id_type=MESH,
        )

    def to_core():
        for quarter in range(4):
            for block in range(4 * quarter, 4 * quarter + 4):

                @pl.when(block != mine)
                def _():
                    chip_copy(quarter, chip, block).wait_recv()

            core_copy(core, quarter).start()

    for load in loads[1:]:
        load.wait()
    to_detector.wait_recv()

    to_pair = Exchange("tm", PLANES, 8, CHUNKS, x2, x3, c_send.at[0], c_recv.at[0])
    from_pair = Exchange("tm", PLANES, 8, CHUNKS, x8, x9, c_send.at[1], c_recv.at[1])

    samples_of = split(x1[...])
    for half in range(2):
        parts = []
        for offset in (128 * half, 256 + 128 * half):
            rows = slice(offset, offset + 128)
            parts.append(product((t_first_high[rows], t_first_low[rows]), samples_of, (1, 0)))
        real, imag = parts
        rows = slice(128 * half, 128 * half + 128)
        cos, sin = t_cos[rows], t_sin[rows]
        turned = jnp.concatenate([real * cos + imag * sin, imag * cos - real * sin], axis=1)
        bins = product((t_second_high[...], t_second_low[...]), split(turned), (1, 1))
        for p in range(PLANES):
            x2[32 * p + 16 * half : 32 * p + 16 * half + 16, :] = bins[16 * p : 16 * p + 16]
        to_pair.start(2 * half)
        to_pair.start(2 * half + 1)

    @pl.when(leaves)
    def _():
        each_quarter(mine, lambda quarter: part_copy(quarter, sent, part_from).wait_recv())

    @pl.when(stays)
    def _():
        part_stays.wait()

    each_quarter(mine, to_chips)

    def bins_copy(n, source, target, peer):
        pltpu.make_async_remote_copy(
            src_ref=source.at[rows_at(peer, 16)],
            dst_ref=target.at[rows_at(group, 16)],
            send_sem=d_send.at[n],
            recv_sem=d_recv.at[n * CHUNKS + (kind if n else 0)],
            device_id={"det": peer},
            device_id_type=MESH,
        ).start()

    def spread(chunk):
        to_pair.wait_recv(chunk)
        for u in range(8):
            x4[rows_at(4 * u + chunk, 16)] = x3[pl.ds(8 * chunk + u, PLANES, stride=32), :]

        for u in (4, 3, 5, 2, 6, 1, 7):
            bins_copy(0, x4, x5, 4 * lax.rem(group // 4 + u, 8) + chunk)

        @pl.when(kind != chunk)
        def _():
            bins_copy(0, x4, x5, 4 * (group // 4) + chunk)

        @pl.when(kind == chunk)
        def _():
            x5[rows_at(group, 16)] = x4[rows_at(group, 16)]

    def factor_ready():
        for quarter in range(4):
            core_copy(1 - core, quarter).wait_recv()
            rows = slice(128 * quarter, 128 * quarter + 128)
            depth = 128 * quarter + 128
            block = gathered[4 * quarter : 4 * quarter + 4, :, :depth]
            high, low = split(block.reshape(128, depth))
            factor_high[rows, :depth] = high
            factor_low[rows, :depth] = low

    def mix():
        await_rows(x5.at[0 : DETS - 16], d_recv.at[0])
        high, low = split(x5[...])
        for quarter in range(4):
            rows = slice(128 * quarter, 128 * quarter + 128)
            depth = 128 * quarter + 128
            x6[rows] = product(
                (factor_high[rows, :depth], factor_low[rows, :depth]), (high[:depth], low[:depth]), (1, 0)
            )
            for u in range(1, 8):
                bins_copy(1, x6, x7, 8 * quarter + lax.rem(group + u, 8))

            @pl.when(group // 8 != quarter)
            def _():
                bins_copy(1, x6, x7, 8 * quarter + lax.rem(group, 8))

        x7[rows_at(group, 16)] = x6[rows_at(group, 16)]

    def gather(chunk):
        @pl.when(kind == chunk)
        def _():
            await_rows(x7.at[0:112], d_recv.at[CHUNKS + chunk])

        @pl.when(kind != chunk)
        def _():
            await_rows(x7.at[0:128], d_recv.at[CHUNKS + chunk])

        for u in range(8):
            x8[pl.ds(8 * chunk + u, PLANES, stride=32), :] = x7[rows_at(4 * u + chunk, 16)]
        from_pair.start(chunk)

    def stage(n, carry):
        @pl.when(n < CHUNKS)
        def _():
            spread(n)

        @pl.when(n == 0)
        def _():
            to_core()

        @pl.when(n == 1)
        def _():
            factor_ready()

        @pl.when(kind == n - 1)
        def _():
            mix()

        @pl.when(n >= 3)
        def _():
            gather(n - 3)

        return carry

    lax.fori_loop(0, CHUNKS + 3, stage, 0)

    for half in range(2):
        from_pair.wait_recv(2 * half)
        from_pair.wait_recv(2 * half + 1)
        for p in range(PLANES):
            flat[16 * p : 16 * p + 16] = x9[32 * p + 16 * half : 32 * p + 16 * half + 16, :]
        back = product(split(flat[...]), (t_second_high[...], t_second_low[...]), (0, 0))
        real, imag = back[:, :LANES], back[:, LANES:]
        rows = slice(128 * half, 128 * half + 128)
        cos, sin = t_cos[rows], t_sin[rows]
        for offset, turned in (
            (128 * half, real * cos - imag * sin),
            (256 + 128 * half, imag * cos + real * sin),
        ):
            high, low = split(turned * (2.0 / TOTAL))
            turned_high[offset : offset + 128] = high
            turned_low[offset : offset + 128] = low
    x10[...] = product(
        (t_first_high[...], t_first_low[...]), (turned_high[...], turned_low[...]), (0, 0)
    )

    to_block = Exchange("tm", PLANES, 32, 1, x10, x11, z_send.at[1], z_recv.at[pl.ds(1, 1)])
    to_block.start()
    to_block.wait_recv()
    for j in range(32):
        out[:, LANES * j : LANES * (j + 1)] = x11[pl.ds(j, PLANES, stride=32), :]

    @pl.when(leaves)
    def _():
        each_quarter(plane, lambda quarter: part_copy(quarter, sent, part_to).wait_send())

    each_quarter(
        mine, lambda quarter: await_rows(gathered.at[0:15, 0:16, 0 : 128 * quarter + 128], f_send)
    )
    for quarter in range(4):
        core_copy(core, quarter).wait_send()
    await_rows(x4.at[0 : DETS - 16], d_send.at[0])
    await_rows(x6.at[0 : DETS - 16], d_send.at[1])
    for exchange in (to_detector, to_pair, from_pair, to_block):
        exchange.wait_send()


def local(noise, factor):
    any_space = pl.BlockSpec(memory_space=pl.ANY)
    block = pltpu.VMEM((ROWS, LANES), f32)
    return pl.pallas_call(
        kernel,
        out_shape=jax.ShapeDtypeStruct((PLANES, ROWS * LANES // PLANES), f32),
        in_specs=[any_space] * 8,
        out_specs=pl.BlockSpec(memory_space=pltpu.VMEM),
        scratch_shapes=[
            pltpu.VMEM((PLANES, ROWS * LANES // PLANES), f32),
            *[block] * 12,
            pltpu.VMEM((256, LANES), f32),
            pltpu.VMEM((ROWS, LANES), bf16),
            pltpu.VMEM((ROWS, LANES), bf16),
            pltpu.VMEM((16, 32, DETS), f32),
            pltpu.VMEM((DETS, DETS), bf16),
            pltpu.VMEM((DETS, DETS), bf16),
            pltpu.VMEM((512, 512), bf16),
            pltpu.VMEM((512, 512), bf16),
            pltpu.VMEM((256, 256), bf16),
            pltpu.VMEM((256, 256), bf16),
            pltpu.VMEM((256, LANES), f32),
            pltpu.VMEM((256, LANES), f32),
            pltpu.SemaphoreType.DMA((2,)),
            pltpu.SemaphoreType.DMA((2,)),
            pltpu.SemaphoreType.DMA((2,)),
            pltpu.SemaphoreType.DMA((2, CHUNKS)),
            pltpu.SemaphoreType.DMA((2,)),
            pltpu.SemaphoreType.DMA((2 * CHUNKS,)),
            pltpu.SemaphoreType.DMA,
            pltpu.SemaphoreType.DMA((16,)),
            pltpu.SemaphoreType.DMA((4,)),
            pltpu.SemaphoreType.DMA((4,)),
            pltpu.SemaphoreType.DMA,
            pltpu.SemaphoreType.DMA,
            pltpu.SemaphoreType.DMA((8,)),
        ],
        compiler_params=pltpu.CompilerParams(collective_id=0, has_side_effects=True),
        name="mix",
    )(noise, factor, *make_tables())


def solution(mesh):
    in_specs = (P("det", "tm"), P("det", "tm", None))
    return jax.shard_map(local, mesh=mesh, in_specs=in_specs, out_specs=P("det", "tm"), check_vma=False)
```

```python
import math

import jax
import jax.numpy as jnp
import numpy as np
from jax import lax
from jax.experimental import pallas as pl
from jax.experimental.pallas import tpu as pltpu
from jax.sharding import PartitionSpec as P

MESH = pl.DeviceIdType.MESH
f32, bf16 = jnp.float32, jnp.bfloat16

PLANES = 16
GROUPS = 32
LANES = 128
ROWS = 512
DETS = 512
TOTAL = 65536
CHUNKS = 4


def split(values):
    high = values.astype(bf16)
    return high, (values - high.astype(f32)).astype(bf16)


def table_parts(table):
    high = table.astype(bf16)
    return high, (table - high.astype(np.float64)).astype(bf16)


def make_tables():
    q = np.arange(256)[:, None] + 0.5
    first = 2.0 * math.pi / 512 * (q * np.arange(512)[None, :])
    first = np.concatenate([np.cos(first), -np.sin(first)], axis=0)
    turn = 2.0 * math.pi / TOTAL * (q * np.arange(LANES)[None, :])
    pair = np.arange(16)[:, None]
    place = np.arange(4)[None, :]
    m = np.concatenate([4 * pair + place, 4 * (31 - pair) + place], axis=1)
    second = 2.0 * math.pi / LANES * ((m[:, :, None] * np.arange(LANES)) % LANES)
    cosines, sines = np.cos(second), np.sin(second)
    real_rows = np.concatenate([cosines, sines], axis=2)
    imag_rows = np.concatenate([-sines, cosines], axis=2)
    second = np.concatenate([real_rows, imag_rows], axis=1).reshape(256, 256)
    return (
        *table_parts(first),
        *table_parts(second),
        np.cos(turn).astype(np.float32),
        np.sin(turn).astype(np.float32),
    )


def product(left, right, dims):
    numbers = ((dims[:1], dims[1:]), ((), ()))
    total = None
    for a, b in ((0, 1), (1, 0), (0, 0)):
        term = lax.dot_general(left[a], right[b], numbers, preferred_element_type=f32)
        total = term if total is None else total + term
    return total


def rows_at(index, count):
    return pl.ds(pl.multiple_of(index * count, count), count)


def away(step, count):
    return count // 2 + (step + 1) // 2 * (1 - 2 * (step % 2))


def await_rows(ref, sem):
    pltpu.make_async_copy(ref, ref, sem).wait()


class Exchange:
    def __init__(self, axis, count, rows, chunks, source, target, send, recv):
        self.axis, self.count, self.rows, self.chunks = axis, count, rows, chunks
        self.source, self.target, self.send, self.recv = source, target, send, recv

    def start(self, chunk=0):
        me = lax.axis_index(self.axis)
        here = rows_at(me * self.chunks + chunk, self.rows)

        def step(k, carry):
            peer = lax.rem(me + away(k, self.count), self.count)
            pltpu.make_async_remote_copy(
                src_ref=self.source.at[rows_at(peer * self.chunks + chunk, self.rows)],
                dst_ref=self.target.at[here],
                send_sem=self.send,
                recv_sem=self.recv.at[chunk],
                device_id={self.axis: peer},
                device_id_type=MESH,
            ).start()
            return carry

        lax.fori_loop(0, self.count - 1, step, 0, unroll=True)
        self.target[here] = self.source[here]

    def send_to(self, peer):
        me = lax.axis_index(self.axis)
        pltpu.make_async_remote_copy(
            src_ref=self.source.at[rows_at(peer, self.rows)],
            dst_ref=self.target.at[rows_at(me, self.rows)],
            send_sem=self.send,
            recv_sem=self.recv.at[0],
            device_id={self.axis: peer},
            device_id_type=MESH,
        ).start()

    def wait_recv(self, chunk=0):
        await_rows(self.target.at[0 : (self.count - 1) * self.rows], self.recv.at[chunk])

    def wait_send(self):
        await_rows(self.source.at[0 : (self.count - 1) * self.rows * self.chunks], self.send)


def kernel(
    noise, factor, first_high, first_low, second_high, second_low, cosines, sines, out,
    samples, x0, x1, x2, x3, x4, x5, x6, x7, x8, x9, x10, x11, flat, turned_high, turned_low, gathered, factor_high, factor_low,
    t_first_high, t_first_low, t_second_high, t_second_low, t_cos, t_sin,
    z_send, z_recv, c_send, c_recv, d_send, d_recv, f_send, f_recv, twin_send, twin_recv, part_send, part_recv, local_sem,
):
    plane = lax.axis_index("tm")
    group = lax.axis_index("det")
    upper = group // 16
    core = lax.rem(group, 2)
    chip = group // 2
    kind = lax.rem(group, CHUNKS)
    pair = group + upper * (31 - 2 * group)
    sent = 2 * plane + upper
    part_to = (pair, 2 * lax.rem(plane + pair, PLANES) + upper)
    mine = lax.rem(chip - plane + PLANES, PLANES)
    part_from = (mine, plane + core * (31 - 2 * plane))
    stays = jnp.logical_and(part_to[0] == plane, part_to[1] == group)
    leaves = jnp.logical_not(stays)

    loads = [pltpu.make_async_copy(noise, samples, local_sem.at[0])]
    tables = (
        (first_high, t_first_high), (first_low, t_first_low), (second_high, t_second_high),
        (second_low, t_second_low), (cosines, t_cos), (sines, t_sin),
    )
    for n, (source, target) in enumerate(tables):
        loads.append(pltpu.make_async_copy(source, target, local_sem.at[n + 1]))
    loads[0].start()

    barrier = pltpu.get_barrier_semaphore()

    def greet_planes(k, carry):
        peer = lax.rem(plane + away(k, PLANES), PLANES)
        pl.semaphore_signal(barrier, inc=1, device_id={"tm": peer}, device_id_type=MESH)
        return carry

    def greet_groups(k, carry):
        peer = lax.rem(group + away(k, GROUPS), GROUPS)
        pl.semaphore_signal(barrier, inc=1, device_id={"det": peer}, device_id_type=MESH)
        return carry

    lax.fori_loop(0, PLANES - 1, greet_planes, 0, unroll=True)

    @pl.when(leaves)
    def _():
        for other in (part_to, part_from):
            pl.semaphore_signal(
                barrier, inc=1, device_id={"tm": other[0], "det": other[1]}, device_id_type=MESH
            )

    lax.fori_loop(0, GROUPS - 1, greet_groups, 0, unroll=True)
    for load in loads[1:]:
        load.start()

    loads[0].wait()
    for j in range(32):
        x0[pl.ds(j, PLANES, stride=32), :] = samples[:, LANES * j : LANES * (j + 1)]

    @pl.when(stays)
    def _():
        pl.semaphore_wait(barrier, PLANES + GROUPS - 2)

    @pl.when(leaves)
    def _():
        pl.semaphore_wait(barrier, PLANES + GROUPS)

    to_detector = Exchange("tm", PLANES, 32, 1, x0, x1, z_send.at[0], z_recv.at[pl.ds(0, 1)])
    to_detector.start()

    part = factor.at[0, pl.ds(pl.multiple_of(16 * upper, 16), 16)]

    def factor_block(index):
        return gathered.at[index // 2, pl.ds(pl.multiple_of(16 * lax.rem(index, 2), 16), 16)]

    def part_copy(quarter, index, other):
        columns = pl.ds(0, 128 * quarter + 128)
        return pltpu.make_async_remote_copy(
            src_ref=part.at[:, columns],
            dst_ref=factor_block(index).at[:, columns],
            send_sem=part_send,
            recv_sem=part_recv,
            device_id={"tm": other[0], "det": other[1]},
            device_id_type=MESH,
        )

    part_stays = pltpu.make_async_copy(part, factor_block(sent), part_recv)

    def each_quarter(of, action):
        for quarter in range(4):

            @pl.when(of // 4 == quarter)
            def _():
                action(quarter)

    @pl.when(leaves)
    def _():
        each_quarter(plane, lambda quarter: part_copy(quarter, sent, part_to).start())

    @pl.when(stays)
    def _():
        part_stays.start()

    def chip_copy(quarter, other, block):
        columns = pl.ds(0, 128 * quarter + 128)
        return pltpu.make_async_remote_copy(
            src_ref=factor_block(2 * block + core).at[:, columns],
            dst_ref=factor_block(2 * block + core).at[:, columns],
            send_sem=f_send,
            recv_sem=f_recv.at[block],
            device_id={"det": 2 * other + core},
            device_id_type=MESH,
        )

    def to_chips(quarter):
        def step(k, carry):
            chip_copy(quarter, lax.rem(chip + away(k, 16), 16), mine).start()
            return carry

        lax.fori_loop(0, 15, step, 0)

    def core_copy(half, quarter):
        ref = gathered.at[
            4 * quarter : 4 * quarter + 4,
            pl.ds(pl.multiple_of(16 * half, 16), 16),
            0 : 128 * quarter + 128,
        ]
        return pltpu.make_async_remote_copy(
            src_ref=ref,
            dst_ref=ref,
            send_sem=twin_send.at[quarter],
            recv_sem=twin_recv.at[quarter],
            device_id={"det": group + 1 - 2 * core},
            device_id_type=MESH,
        )

    def to_core():
        for quarter in range(4):
            for block in range(4 * quarter, 4 * quarter + 4):

                @pl.when(block != mine)
                def _():
                    chip_copy(quarter, chip, block).wait_recv()

            core_copy(core, quarter).start()

    for load in loads[1:]:
        load.wait()
    to_detector.wait_recv()

    to_pair = Exchange("tm", PLANES, 8, CHUNKS, x2, x3, c_send.at[0], c_recv.at[0])
    from_pair = Exchange("tm", PLANES, 8, CHUNKS, x8, x9, c_send.at[1], c_recv.at[1])

    samples_of = split(x1[...])
    for half in range(2):
        parts = []
        for offset in (128 * half, 256 + 128 * half):
            rows = slice(offset, offset + 128)
            parts.append(product((t_first_high[rows], t_first_low[rows]), samples_of, (1, 0)))
        real, imag = parts
        rows = slice(128 * half, 128 * half + 128)
        cos, sin = t_cos[rows], t_sin[rows]
        turned = jnp.concatenate([real * cos + imag * sin, imag * cos - real * sin], axis=1)
        bins = product((t_second_high[...], t_second_low[...]), split(turned), (1, 1))
        for p in range(PLANES):
            x2[32 * p + 16 * half : 32 * p + 16 * half + 16, :] = bins[16 * p : 16 * p + 16]
        to_pair.start(2 * half)
        to_pair.start(2 * half + 1)

    @pl.when(leaves)
    def _():
        each_quarter(mine, lambda quarter: part_copy(quarter, sent, part_from).wait_recv())

    @pl.when(stays)
    def _():
        part_stays.wait()

    each_quarter(mine, to_chips)

    def bins_copy(n, source, target, peer):
        pltpu.make_async_remote_copy(
            src_ref=source.at[rows_at(peer, 16)],
            dst_ref=target.at[rows_at(group, 16)],
            send_sem=d_send.at[n],
            recv_sem=d_recv.at[n * CHUNKS + (kind if n else 0)],
            device_id={"det": peer},
            device_id_type=MESH,
        ).start()

    def spread(chunk):
        to_pair.wait_recv(chunk)
        for u in range(8):
            x4[rows_at(4 * u + chunk, 16)] = x3[pl.ds(8 * chunk + u, PLANES, stride=32), :]

        for u in (4, 3, 5, 2, 6, 1, 7):
            bins_copy(0, x4, x5, 4 * lax.rem(group // 4 + u, 8) + chunk)

        @pl.when(kind != chunk)
        def _():
            bins_copy(0, x4, x5, 4 * (group // 4) + chunk)

        @pl.when(kind == chunk)
        def _():
            x5[rows_at(group, 16)] = x4[rows_at(group, 16)]

    def factor_ready():
        for quarter in range(4):
            core_copy(1 - core, quarter).wait_recv()
            rows = slice(128 * quarter, 128 * quarter + 128)
            depth = 128 * quarter + 128
            block = gathered[4 * quarter : 4 * quarter + 4, :, :depth]
            high, low = split(block.reshape(128, depth))
            factor_high[rows, :depth] = high
            factor_low[rows, :depth] = low

    def mix():
        await_rows(x5.at[0 : DETS - 16], d_recv.at[0])
        high, low = split(x5[...])
        for quarter in range(4):
            rows = slice(128 * quarter, 128 * quarter + 128)
            depth = 128 * quarter + 128
            x6[rows] = product(
                (factor_high[rows, :depth], factor_low[rows, :depth]), (high[:depth], low[:depth]), (1, 0)
            )
            for u in range(1, 8):
                bins_copy(1, x6, x7, 8 * quarter + lax.rem(group + u, 8))

            @pl.when(group // 8 != quarter)
            def _():
                bins_copy(1, x6, x7, 8 * quarter + lax.rem(group, 8))

        x7[rows_at(group, 16)] = x6[rows_at(group, 16)]

    def gather(chunk):
        @pl.when(kind == chunk)
        def _():
            await_rows(x7.at[0:112], d_recv.at[CHUNKS + chunk])

        @pl.when(kind != chunk)
        def _():
            await_rows(x7.at[0:128], d_recv.at[CHUNKS + chunk])

        for u in range(8):
            x8[pl.ds(8 * chunk + u, PLANES, stride=32), :] = x7[rows_at(4 * u + chunk, 16)]
        from_pair.start(chunk)

    def stage(n, carry):
        @pl.when(n < CHUNKS)
        def _():
            spread(n)

        @pl.when(n == 0)
        def _():
            to_core()

        @pl.when(n == 1)
        def _():
            factor_ready()

        @pl.when(kind == n - 1)
        def _():
            mix()

        @pl.when(n >= 2)
        def _():
            gather(n - 2)

        return carry

    lax.fori_loop(0, CHUNKS + 2, stage, 0)

    for half in range(2):
        from_pair.wait_recv(2 * half)
        from_pair.wait_recv(2 * half + 1)
        for p in range(PLANES):
            flat[16 * p : 16 * p + 16] = x9[32 * p + 16 * half : 32 * p + 16 * half + 16, :]
        back = product(split(flat[...]), (t_second_high[...], t_second_low[...]), (0, 0))
        real, imag = back[:, :LANES], back[:, LANES:]
        rows = slice(128 * half, 128 * half + 128)
        cos, sin = t_cos[rows], t_sin[rows]
        for offset, turned in (
            (128 * half, real * cos - imag * sin),
            (256 + 128 * half, imag * cos + real * sin),
        ):
            high, low = split(turned * (2.0 / TOTAL))
            turned_high[offset : offset + 128] = high
            turned_low[offset : offset + 128] = low
    to_block = Exchange("tm", PLANES, 32, 1, x10, x11, z_send.at[1], z_recv.at[pl.ds(1, 1)])
    turned = (turned_high[...], turned_low[...])
    for step in (2, 1, 3, 0):
        quarter = lax.rem(plane // 4 + step, 4)
        columns = pl.ds(pl.multiple_of(LANES * quarter, LANES), LANES)
        x10[rows_at(quarter, LANES)] = product(
            (t_first_high[:, columns], t_first_low[:, columns]), turned, (0, 0)
        )
        for place in (2, 1, 3, 0):
            if step or place:
                to_block.send_to(4 * quarter + lax.rem(plane + place, 4))
    x11[rows_at(plane, 32)] = x10[rows_at(plane, 32)]
    to_block.wait_recv()
    for j in range(32):
        out[:, LANES * j : LANES * (j + 1)] = x11[pl.ds(j, PLANES, stride=32), :]

    @pl.when(leaves)
    def _():
        each_quarter(plane, lambda quarter: part_copy(quarter, sent, part_to).wait_send())

    each_quarter(
        mine, lambda quarter: await_rows(gathered.at[0:15, 0:16, 0 : 128 * quarter + 128], f_send)
    )
    for quarter in range(4):
        core_copy(core, quarter).wait_send()
    await_rows(x4.at[0 : DETS - 16], d_send.at[0])
    await_rows(x6.at[0 : DETS - 16], d_send.at[1])
    for exchange in (to_detector, to_pair, from_pair, to_block):
        exchange.wait_send()


def local(noise, factor):
    any_space = pl.BlockSpec(memory_space=pl.ANY)
    block = pltpu.VMEM((ROWS, LANES), f32)
    return pl.pallas_call(
        kernel,
        out_shape=jax.ShapeDtypeStruct((PLANES, ROWS * LANES // PLANES), f32),
        in_specs=[any_space] * 8,
        out_specs=pl.BlockSpec(memory_space=pltpu.VMEM),
        scratch_shapes=[
            pltpu.VMEM((PLANES, ROWS * LANES // PLANES), f32),
            *[block] * 12,
            pltpu.VMEM((256, LANES), f32),
            pltpu.VMEM((ROWS, LANES), bf16),
            pltpu.VMEM((ROWS, LANES), bf16),
            pltpu.VMEM((16, 32, DETS), f32),
            pltpu.VMEM((DETS, DETS), bf16),
            pltpu.VMEM((DETS, DETS), bf16),
            pltpu.VMEM((512, 512), bf16),
            pltpu.VMEM((512, 512), bf16),
            pltpu.VMEM((256, 256), bf16),
            pltpu.VMEM((256, 256), bf16),
            pltpu.VMEM((256, LANES), f32),
            pltpu.VMEM((256, LANES), f32),
            pltpu.SemaphoreType.DMA((2,)),
            pltpu.SemaphoreType.DMA((2,)),
            pltpu.SemaphoreType.DMA((2,)),
            pltpu.SemaphoreType.DMA((2, CHUNKS)),
            pltpu.SemaphoreType.DMA((2,)),
            pltpu.SemaphoreType.DMA((2 * CHUNKS,)),
            pltpu.SemaphoreType.DMA,
            pltpu.SemaphoreType.DMA((16,)),
            pltpu.SemaphoreType.DMA((4,)),
            pltpu.SemaphoreType.DMA((4,)),
            pltpu.SemaphoreType.DMA,
            pltpu.SemaphoreType.DMA,
            pltpu.SemaphoreType.DMA((8,)),
        ],
        compiler_params=pltpu.CompilerParams(collective_id=0, has_side_effects=True),
        name="mix",
    )(noise, factor, *make_tables())


def solution(mesh):
    in_specs = (P("det", "tm"), P("det", "tm", None))
    return jax.shard_map(local, mesh=mesh, in_specs=in_specs, out_specs=P("det", "tm"), check_vma=False)
```

```python
import math

import jax
import jax.numpy as jnp
import numpy as np
from jax import lax
from jax.experimental import pallas as pl
from jax.experimental.pallas import tpu as pltpu
from jax.sharding import PartitionSpec as P

MESH = pl.DeviceIdType.MESH
f32, bf16 = jnp.float32, jnp.bfloat16

PLANES = 16
GROUPS = 32
LANES = 128
ROWS = 512
DETS = 512
TOTAL = 65536
CHUNKS = 4


def split(values):
    high = values.astype(bf16)
    return high, (values - high.astype(f32)).astype(bf16)


def table_parts(table):
    high = table.astype(bf16)
    return high, (table - high.astype(np.float64)).astype(bf16)


def make_tables():
    q = np.arange(256)[:, None] + 0.5
    first = 2.0 * math.pi / 512 * (q * np.arange(512)[None, :])
    first = np.concatenate([np.cos(first), -np.sin(first)], axis=0)
    turn = 2.0 * math.pi / TOTAL * (q * np.arange(LANES)[None, :])
    pair = np.arange(16)[:, None]
    place = np.arange(4)[None, :]
    m = np.concatenate([4 * pair + place, 4 * (31 - pair) + place], axis=1)
    second = 2.0 * math.pi / LANES * ((m[:, :, None] * np.arange(LANES)) % LANES)
    cosines, sines = np.cos(second), np.sin(second)
    real_rows = np.concatenate([cosines, sines], axis=2)
    imag_rows = np.concatenate([-sines, cosines], axis=2)
    second = np.concatenate([real_rows, imag_rows], axis=1).reshape(256, 256)
    return (
        *table_parts(first),
        *table_parts(second),
        np.cos(turn).astype(np.float32),
        np.sin(turn).astype(np.float32),
    )


def product(left, right, dims):
    numbers = ((dims[:1], dims[1:]), ((), ()))
    total = None
    for a, b in ((0, 1), (1, 0), (0, 0)):
        term = lax.dot_general(left[a], right[b], numbers, preferred_element_type=f32)
        total = term if total is None else total + term
    return total


def rows_at(index, count):
    return pl.ds(pl.multiple_of(index * count, count), count)


def away(step, count):
    return count // 2 + (step + 1) // 2 * (1 - 2 * (step % 2))


def await_rows(ref, sem):
    pltpu.make_async_copy(ref, ref, sem).wait()


class Exchange:
    def __init__(self, axis, count, rows, chunks, source, target, send, recv):
        self.axis, self.count, self.rows, self.chunks = axis, count, rows, chunks
        self.source, self.target, self.send, self.recv = source, target, send, recv

    def start(self, chunk=0):
        me = lax.axis_index(self.axis)
        here = rows_at(me * self.chunks + chunk, self.rows)

        def step(k, carry):
            peer = lax.rem(me + away(k, self.count), self.count)
            pltpu.make_async_remote_copy(
                src_ref=self.source.at[rows_at(peer * self.chunks + chunk, self.rows)],
                dst_ref=self.target.at[here],
                send_sem=self.send,
                recv_sem=self.recv.at[chunk],
                device_id={self.axis: peer},
                device_id_type=MESH,
            ).start()
            return carry

        lax.fori_loop(0, self.count - 1, step, 0, unroll=True)
        self.target[here] = self.source[here]

    def wait_recv(self, chunk=0):
        await_rows(self.target.at[0 : (self.count - 1) * self.rows], self.recv.at[chunk])

    def wait_send(self):
        await_rows(self.source.at[0 : (self.count - 1) * self.rows * self.chunks], self.send)


def kernel(
    noise, factor, first_high, first_low, second_high, second_low, cosines, sines, out,
    samples, x0, x1, x2, x3, x4, x5, x6, x7, x8, x9, x10, x11, flat, turned_high, turned_low, gathered, factor_high, factor_low,
    t_first_high, t_first_low, t_second_high, t_second_low, t_cos, t_sin,
    z_send, z_recv, c_send, c_recv, d_send, d_recv, f_send, f_recv, twin_send, twin_recv, part_send, part_recv, local_sem,
):
    plane = lax.axis_index("tm")
    group = lax.axis_index("det")
    upper = group // 16
    core = lax.rem(group, 2)
    chip = group // 2
    kind = lax.rem(group, CHUNKS)
    pair = group + upper * (31 - 2 * group)
    sent = 2 * plane + upper
    part_to = (pair, 2 * lax.rem(plane + pair, PLANES) + upper)
    mine = lax.rem(chip - plane + PLANES, PLANES)
    part_from = (mine, plane + core * (31 - 2 * plane))
    stays = jnp.logical_and(part_to[0] == plane, part_to[1] == group)
    leaves = jnp.logical_not(stays)

    loads = [pltpu.make_async_copy(noise, samples, local_sem.at[0])]
    tables = (
        (first_high, t_first_high), (first_low, t_first_low), (second_high, t_second_high),
        (second_low, t_second_low), (cosines, t_cos), (sines, t_sin),
    )
    for n, (source, target) in enumerate(tables):
        loads.append(pltpu.make_async_copy(source, target, local_sem.at[n + 1]))
    loads[0].start()

    barrier = pltpu.get_barrier_semaphore()

    def greet_planes(k, carry):
        peer = lax.rem(plane + away(k, PLANES), PLANES)
        pl.semaphore_signal(barrier, inc=1, device_id={"tm": peer}, device_id_type=MESH)
        return carry

    def greet_groups(k, carry):
        peer = lax.rem(group + away(k, GROUPS), GROUPS)
        pl.semaphore_signal(barrier, inc=1, device_id={"det": peer}, device_id_type=MESH)
        return carry

    lax.fori_loop(0, PLANES - 1, greet_planes, 0, unroll=True)

    @pl.when(leaves)
    def _():
        for other in (part_to, part_from):
            pl.semaphore_signal(
                barrier, inc=1, device_id={"tm": other[0], "det": other[1]}, device_id_type=MESH
            )

    lax.fori_loop(0, GROUPS - 1, greet_groups, 0, unroll=True)
    for load in loads[1:]:
        load.start()

    loads[0].wait()
    for j in range(32):
        x0[pl.ds(j, PLANES, stride=32), :] = samples[:, LANES * j : LANES * (j + 1)]

    @pl.when(stays)
    def _():
        pl.semaphore_wait(barrier, PLANES + GROUPS - 2)

    @pl.when(leaves)
    def _():
        pl.semaphore_wait(barrier, PLANES + GROUPS)

    to_detector = Exchange("tm", PLANES, 32, 1, x0, x1, z_send.at[0], z_recv.at[pl.ds(0, 1)])
    to_detector.start()

    part = factor.at[0, pl.ds(pl.multiple_of(16 * upper, 16), 16)]

    def factor_block(index):
        return gathered.at[index // 2, pl.ds(pl.multiple_of(16 * lax.rem(index, 2), 16), 16)]

    def part_copy(quarter, index, other):
        columns = pl.ds(0, 128 * quarter + 128)
        return pltpu.make_async_remote_copy(
            src_ref=part.at[:, columns],
            dst_ref=factor_block(index).at[:, columns],
            send_sem=part_send,
            recv_sem=part_recv,
            device_id={"tm": other[0], "det": other[1]},
            device_id_type=MESH,
        )

    part_stays = pltpu.make_async_copy(part, factor_block(sent), part_recv)

    def each_quarter(of, action):
        for quarter in range(4):

            @pl.when(of // 4 == quarter)
            def _():
                action(quarter)

    @pl.when(leaves)
    def _():
        each_quarter(plane, lambda quarter: part_copy(quarter, sent, part_to).start())

    @pl.when(stays)
    def _():
        part_stays.start()

    def chip_copy(quarter, other, block):
        columns = pl.ds(0, 128 * quarter + 128)
        return pltpu.make_async_remote_copy(
            src_ref=factor_block(2 * block + core).at[:, columns],
            dst_ref=factor_block(2 * block + core).at[:, columns],
            send_sem=f_send,
            recv_sem=f_recv.at[block],
            device_id={"det": 2 * other + core},
            device_id_type=MESH,
        )

    def to_chips(quarter):
        def step(k, carry):
            chip_copy(quarter, lax.rem(chip + away(k, 16), 16), mine).start()
            return carry

        lax.fori_loop(0, 15, step, 0)

    def core_copy(half, quarter):
        ref = gathered.at[
            4 * quarter : 4 * quarter + 4,
            pl.ds(pl.multiple_of(16 * half, 16), 16),
            0 : 128 * quarter + 128,
        ]
        return pltpu.make_async_remote_copy(
            src_ref=ref,
            dst_ref=ref,
            send_sem=twin_send.at[quarter],
            recv_sem=twin_recv.at[quarter],
            device_id={"det": group + 1 - 2 * core},
            device_id_type=MESH,
        )

    def to_core():
        for quarter in range(4):
            for block in range(4 * quarter, 4 * quarter + 4):

                @pl.when(block != mine)
                def _():
                    chip_copy(quarter, chip, block).wait_recv()

            core_copy(core, quarter).start()

    for load in loads[1:]:
        load.wait()
    to_detector.wait_recv()

    to_pair = Exchange("tm", PLANES, 8, CHUNKS, x2, x3, c_send.at[0], c_recv.at[0])
    from_pair = Exchange("tm", PLANES, 8, CHUNKS, x8, x9, c_send.at[1], c_recv.at[1])

    samples_of = split(x1[...])
    for half in range(2):
        parts = []
        for offset in (128 * half, 256 + 128 * half):
            rows = slice(offset, offset + 128)
            parts.append(product((t_first_high[rows], t_first_low[rows]), samples_of, (1, 0)))
        real, imag = parts
        rows = slice(128 * half, 128 * half + 128)
        cos, sin = t_cos[rows], t_sin[rows]
        turned = jnp.concatenate([real * cos + imag * sin, imag * cos - real * sin], axis=1)
        bins = product((t_second_high[...], t_second_low[...]), split(turned), (1, 1))
        for p in range(PLANES):
            x2[32 * p + 16 * half : 32 * p + 16 * half + 16, :] = bins[16 * p : 16 * p + 16]
        to_pair.start(2 * half)
        to_pair.start(2 * half + 1)

    @pl.when(leaves)
    def _():
        each_quarter(mine, lambda quarter: part_copy(quarter, sent, part_from).wait_recv())

    @pl.when(stays)
    def _():
        part_stays.wait()

    each_quarter(mine, to_chips)

    def bins_copy(n, source, target, peer):
        pltpu.make_async_remote_copy(
            src_ref=source.at[rows_at(peer, 16)],
            dst_ref=target.at[rows_at(group, 16)],
            send_sem=d_send.at[n],
            recv_sem=d_recv.at[n * CHUNKS + (kind if n else 0)],
            device_id={"det": peer},
            device_id_type=MESH,
        ).start()

    def spread(chunk):
        to_pair.wait_recv(chunk)
        for u in range(8):
            x4[rows_at(4 * u + chunk, 16)] = x3[pl.ds(8 * chunk + u, PLANES, stride=32), :]

        for u in (4, 3, 5, 2, 6, 1, 7):
            bins_copy(0, x4, x5, 4 * lax.rem(group // 4 + u, 8) + chunk)

        @pl.when(kind != chunk)
        def _():
            bins_copy(0, x4, x5, 4 * (group // 4) + chunk)

        @pl.when(kind == chunk)
        def _():
            x5[rows_at(group, 16)] = x4[rows_at(group, 16)]

    def factor_ready():
        for quarter in range(4):
            core_copy(1 - core, quarter).wait_recv()
            rows = slice(128 * quarter, 128 * quarter + 128)
            depth = 128 * quarter + 128
            block = gathered[4 * quarter : 4 * quarter + 4, :, :depth]
            high, low = split(block.reshape(128, depth))
            factor_high[rows, :depth] = high
            factor_low[rows, :depth] = low

    def mix():
        await_rows(x5.at[0 : DETS - 16], d_recv.at[0])
        high, low = split(x5[...])
        for quarter in range(4):
            rows = slice(128 * quarter, 128 * quarter + 128)
            depth = 128 * quarter + 128
            x6[rows] = product(
                (factor_high[rows, :depth], factor_low[rows, :depth]), (high[:depth], low[:depth]), (1, 0)
            )
            for u in range(1, 8):
                bins_copy(1, x6, x7, 8 * quarter + lax.rem(group + u, 8))

            @pl.when(group // 8 != quarter)
            def _():
                bins_copy(1, x6, x7, 8 * quarter + lax.rem(group, 8))

        x7[rows_at(group, 16)] = x6[rows_at(group, 16)]

    def gather(chunk):
        @pl.when(kind == chunk)
        def _():
            await_rows(x7.at[0:112], d_recv.at[CHUNKS + chunk])

        @pl.when(kind != chunk)
        def _():
            await_rows(x7.at[0:128], d_recv.at[CHUNKS + chunk])

        for u in range(8):
            x8[pl.ds(8 * chunk + u, PLANES, stride=32), :] = x7[rows_at(4 * u + chunk, 16)]
        from_pair.start(chunk)

    def stage(n, carry):
        @pl.when(n < CHUNKS)
        def _():
            spread(n)

        @pl.when(n == 0)
        def _():
            to_core()

        @pl.when(n == 1)
        def _():
            factor_ready()

        @pl.when(kind == n - 1)
        def _():
            mix()

        @pl.when(n >= 2)
        def _():
            gather(n - 2)

        return carry

    lax.fori_loop(0, CHUNKS + 2, stage, 0)

    for half in range(2):
        from_pair.wait_recv(2 * half)
        from_pair.wait_recv(2 * half + 1)
        for p in range(PLANES):
            flat[16 * p : 16 * p + 16] = x9[32 * p + 16 * half : 32 * p + 16 * half + 16, :]
        back = product(split(flat[...]), (t_second_high[...], t_second_low[...]), (0, 0))
        real, imag = back[:, :LANES], back[:, LANES:]
        rows = slice(128 * half, 128 * half + 128)
        cos, sin = t_cos[rows], t_sin[rows]
        for offset, turned in (
            (128 * half, real * cos - imag * sin),
            (256 + 128 * half, imag * cos + real * sin),
        ):
            high, low = split(turned * (2.0 / TOTAL))
            turned_high[offset : offset + 128] = high
            turned_low[offset : offset + 128] = low
    x10[...] = product(
        (t_first_high[...], t_first_low[...]), (turned_high[...], turned_low[...]), (0, 0)
    )

    to_block = Exchange("tm", PLANES, 32, 1, x10, x11, z_send.at[1], z_recv.at[pl.ds(1, 1)])
    to_block.start()
    to_block.wait_recv()
    for j in range(32):
        out[:, LANES * j : LANES * (j + 1)] = x11[pl.ds(j, PLANES, stride=32), :]

    @pl.when(leaves)
    def _():
        each_quarter(plane, lambda quarter: part_copy(quarter, sent, part_to).wait_send())

    each_quarter(
        mine, lambda quarter: await_rows(gathered.at[0:15, 0:16, 0 : 128 * quarter + 128], f_send)
    )
    for quarter in range(4):
        core_copy(core, quarter).wait_send()
    await_rows(x4.at[0 : DETS - 16], d_send.at[0])
    await_rows(x6.at[0 : DETS - 16], d_send.at[1])
    for exchange in (to_detector, to_pair, from_pair, to_block):
        exchange.wait_send()


def local(noise, factor):
    any_space = pl.BlockSpec(memory_space=pl.ANY)
    block = pltpu.VMEM((ROWS, LANES), f32)
    return pl.pallas_call(
        kernel,
        out_shape=jax.ShapeDtypeStruct((PLANES, ROWS * LANES // PLANES), f32),
        in_specs=[any_space] * 8,
        out_specs=pl.BlockSpec(memory_space=pltpu.VMEM),
        scratch_shapes=[
            pltpu.VMEM((PLANES, ROWS * LANES // PLANES), f32),
            *[block] * 12,
            pltpu.VMEM((256, LANES), f32),
            pltpu.VMEM((ROWS, LANES), bf16),
            pltpu.VMEM((ROWS, LANES), bf16),
            pltpu.VMEM((16, 32, DETS), f32),
            pltpu.VMEM((DETS, DETS), bf16),
            pltpu.VMEM((DETS, DETS), bf16),
            pltpu.VMEM((512, 512), bf16),
            pltpu.VMEM((512, 512), bf16),
            pltpu.VMEM((256, 256), bf16),
            pltpu.VMEM((256, 256), bf16),
            pltpu.VMEM((256, LANES), f32),
            pltpu.VMEM((256, LANES), f32),
            pltpu.SemaphoreType.DMA((2,)),
            pltpu.SemaphoreType.DMA((2,)),
            pltpu.SemaphoreType.DMA((2,)),
            pltpu.SemaphoreType.DMA((2, CHUNKS)),
            pltpu.SemaphoreType.DMA((2,)),
            pltpu.SemaphoreType.DMA((2 * CHUNKS,)),
            pltpu.SemaphoreType.DMA,
            pltpu.SemaphoreType.DMA((16,)),
            pltpu.SemaphoreType.DMA((4,)),
            pltpu.SemaphoreType.DMA((4,)),
            pltpu.SemaphoreType.DMA,
            pltpu.SemaphoreType.DMA,
            pltpu.SemaphoreType.DMA((8,)),
        ],
        compiler_params=pltpu.CompilerParams(collective_id=0, has_side_effects=True),
        name="mix",
    )(noise, factor, *make_tables())


def solution(mesh):
    in_specs = (P("det", "tm"), P("det", "tm", None))
    return jax.shard_map(local, mesh=mesh, in_specs=in_specs, out_specs=P("det", "tm"), check_vma=False)
```
